512 devices in a mesh: space: 32 (over z, core), tm: 16 (over y, x).
Axes of the slice: x: 4, y: 4, z: 16, core: 2. Of those that a mesh axis runs over, the one named last changes fastest.
Arguments:
- snapshots: bfloat16 [65536, 16384], P('space', 'tm'), may hold values from -6 to 6
- basis: bfloat16 [65536, 256], P(('space', 'tm')), may hold values from -0.0234375 to 0.0234375
- lengths: int32 [16, 64], P('tm'), may hold values from 1 to 61, as said below
- owners: int32 [16, 64], P('tm'), may hold values from 0 to 31, as said below
Outputs:
- gram_out: bfloat16 [16, 32, 392, 392], P('tm', 'space')
- target_out: bfloat16 [16, 32, 392, 256], P('tm', 'space')
The draws below stay inside these ranges and needn't reach their ends.
Inputs may be any that keep to these rules, and one draw needn't show every extreme that they name: Each row of lengths sums to 1024. The trajectories that one owner holds in one row have 62 snapshots together at most, and in every row some owner holds exactly 62. `owners`: in every row each space index owns exactly two trajectories.
All inputs are finite; a program needn't handle non-finite values.
Results may differ from the reference program's by a relative error of at most 0.0057.
Values may be sent and summed in bfloat16 or wider, within the bound.
No kernel may reach another device: no remote copies, remote signals or barrier semaphores. Data moves between devices by JAX's collectives and lax.ppermute only.
A program may use at most 64 MiB of HBM per device.

```python
import jax
import jax.numpy as jnp
import numpy as np
from jax import lax

R = 256
QM = 16
S_DEV = 1024
CELLS = 65536
SNAPS = 16384
CAP = 62
N_SPACE = 32
N_TM = 16


def plan_row(row_key):
    first_key, pair_key, split_key, order_key = jax.random.split(row_key, 4)
    mean_load = S_DEV // N_SPACE
    half_count = N_SPACE // 2
    spread = jax.random.randint(first_key, (half_count,), 0, mean_load - 1).astype(jnp.int32)
    spread = spread.at[0].set(mean_load - 2)
    pairing = jax.random.permutation(pair_key, N_SPACE)
    pair_loads = jnp.concatenate([mean_load + spread, mean_load - spread]).astype(jnp.int32)
    loads = jnp.zeros((N_SPACE,), jnp.int32).at[pairing].set(pair_loads)
    leading = jax.random.randint(split_key, (N_SPACE,), 1, loads).astype(jnp.int32)
    leading = leading.at[pairing[0]].set(1)
    lengths_all = jnp.concatenate([leading, loads - leading])
    owner_all = jnp.concatenate([jnp.arange(N_SPACE, dtype=jnp.int32), jnp.arange(N_SPACE, dtype=jnp.int32)])
    order = jax.random.permutation(order_key, 2 * N_SPACE)
    return (lengths_all[order], owner_all[order])


def owner_plan(key):
    row_keys = jax.random.split(jax.random.fold_in(key, 11), N_TM)
    return jax.vmap(plan_row)(row_keys)


def draw_lengths(key, part):
    return owner_plan(key)[0]


def draw_owners(key, part):
    return owner_plan(key)[1]


def level_of(own_key, shape, shards, smallest, high):
    def one(axis_at, shards_of):
        steps = jax.random.uniform(jax.random.fold_in(jax.random.fold_in(own_key, 6), axis_at), (shards_of,), jnp.float32, smallest / len(shards), high / len(shards))
        return jnp.repeat(jnp.exp(steps), shape[axis_at] // shards_of).reshape((-1,) + (1,) * (len(shape) - axis_at - 1))

    level = one(*shards[0])
    for cut in shards[1:]:
        level = level * one(*cut)
    return level


def centred(own_key, shape, scale, most, cuts=(), kind=jnp.bfloat16):
    drawn = jax.random.normal(own_key, shape, jnp.float32) * scale
    if len(cuts) > 0:
        drawn = level_of(own_key, shape, cuts, -0.22, 0.18) * drawn
    return jnp.clip(drawn, min=-most, max=most).astype(kind)


def setup_inputs(seed: int = 0) -> dict:
    streams_of = jax.random.split(jax.random.key(seed), 5)
    return {
        "snapshots": centred(streams_of[0], (CELLS, SNAPS), 1.0, 6.0, ((0, 32), (1, 16))),
        "basis": centred(streams_of[1], (CELLS, R), CELLS ** -0.5, 0.0234375, ((0, 512),)),
        "lengths": draw_lengths(jax.random.fold_in(streams_of[4], 71), 0),
        "owners": draw_owners(jax.random.fold_in(streams_of[4], 71), 0),
    }


def slot_plan(length_row, owner_row, owner_count, capacity, snap_count):
    traj_end = jnp.cumsum(length_row).astype(jnp.int32)
    starts = traj_end - length_row
    snap_index = jnp.arange(snap_count, dtype=jnp.int32)
    member = ((snap_index[:, None] >= starts[None, :]) & (snap_index[:, None] < traj_end[None, :])).astype(jnp.int32)
    snap_start = jnp.sum(member * starts[None, :], axis=1)
    snap_end = jnp.sum(member * traj_end[None, :], axis=1)
    snap_owner = jnp.sum(member * owner_row[None, :], axis=1)
    traj_index = jnp.arange(length_row.shape[0], dtype=jnp.int32)
    same_owner = owner_row[:, None] == owner_row[None, :]
    earlier = traj_index[None, :] < traj_index[:, None]
    offset = jnp.sum(jnp.where(same_owner & earlier, length_row[None, :], 0), axis=1).astype(jnp.int32)
    slot_index = jnp.sum(member * offset[None, :], axis=1) + snap_index - snap_start
    has_next = (snap_index + 1 < snap_end).astype(jnp.int32)
    destination = (snap_owner * capacity + slot_index).astype(jnp.int32)
    source_rows = jnp.full((owner_count * capacity,), -1, jnp.int32).at[destination].set(snap_index)
    live_rows = jnp.zeros((owner_count * capacity,), jnp.int32).at[destination].set(has_next)
    return source_rows, live_rows


def library(coords, live_slots, weight_scale):
    first_mode, second_mode = np.triu_indices(QM)
    products = coords[:, first_mode] * coords[:, second_mode]
    library_rows = jnp.concatenate([coords, products], axis=1).astype(jnp.bfloat16)
    successor = jnp.concatenate([coords[1:], jnp.zeros((1, coords.shape[1]), jnp.float32)], axis=0).astype(jnp.bfloat16)
    weighted = library_rows * live_slots[:, None].astype(jnp.bfloat16)
    dims = (((0,), (0,)), ((), ()))
    gram_matrix = lax.dot_general(weighted, library_rows, dims, preferred_element_type=jnp.float32) * weight_scale
    targets = lax.dot_general(weighted, successor, dims, preferred_element_type=jnp.float32) * weight_scale
    return gram_matrix.astype(jnp.bfloat16), targets.astype(jnp.bfloat16)


def reference(snapshots, basis, lengths, owners):
    weight_scale = N_SPACE / S_DEV

    def one_group(group_index):
        columns = lax.dynamic_slice_in_dim(snapshots, group_index * S_DEV, S_DEV, 1)
        coords = lax.dot_general(columns, basis, (((0,), (0,)), ((), ())), preferred_element_type=jnp.float32)
        source_rows, live_rows = slot_plan(lengths[group_index], owners[group_index], N_SPACE, CAP, S_DEV)
        packed = jnp.take(coords, jnp.maximum(source_rows, 0), axis=0) * (source_rows >= 0)[:, None].astype(jnp.float32)
        packed = packed.reshape(N_SPACE, CAP, R)
        live_rows = live_rows.reshape(N_SPACE, CAP)
        return jax.vmap(lambda block, live: library(block, live, weight_scale))(packed, live_rows)

    gram_out, target_out = lax.map(one_group, jnp.arange(N_TM, dtype=jnp.int32))
    return gram_out, target_out
```

```python
import jax
import jax.numpy as jnp
import numpy as np
from jax import lax
from jax.sharding import PartitionSpec as P

QM = 16
SLOTS = 64
f32 = jnp.float32
bf16 = jnp.bfloat16


def plan(length, owner, own, parity, snap_count, chips):
    t = length.shape[0]
    ti = lax.broadcasted_iota(jnp.int32, (t, t), 0)
    tj = lax.broadcasted_iota(jnp.int32, (t, t), 1)
    before = tj < ti
    starts = jnp.sum(jnp.where(before, length[None, :], 0), axis=1)
    same = owner[:, None] == owner[None, :]
    offset = jnp.sum(jnp.where(before & same, length[None, :], 0), axis=1)
    base = jnp.where(
        jnp.bitwise_and(owner, 1) == parity,
        (owner // 2) * SLOTS + offset - starts,
        -2 * snap_count,
    )
    snap = lax.broadcasted_iota(jnp.int32, (t, snap_count), 1)
    member = (snap >= starts[:, None]) & (snap < (starts + length)[:, None])
    shift = jnp.sum(jnp.where(member, base[:, None], 0), axis=0)
    target = shift + jnp.arange(snap_count, dtype=jnp.int32)
    mine = owner == own
    total = jnp.sum(jnp.where(mine, length, 0))
    slot = lax.broadcasted_iota(jnp.int32, (SLOTS, t), 0)
    last = jnp.any(mine[None, :] & (slot == (offset + length - 1)[None, :]), axis=1)
    live = (jnp.arange(SLOTS) < total) & ~last
    return target, live


def library(coords, live, weight_scale):
    first_mode, second_mode = np.triu_indices(QM)
    pick_a = (first_mode[None, :] == lax.broadcasted_iota(jnp.int32, (QM, 1), 0)).astype(f32)
    pick_b = (second_mode[None, :] == lax.broadcasted_iota(jnp.int32, (QM, 1), 0)).astype(f32)
    lead = coords[:, :QM]
    hi = lax.Precision.HIGHEST
    products = jnp.dot(lead, pick_a, precision=hi) * jnp.dot(lead, pick_b, precision=hi)
    rows = jnp.concatenate([coords, products], axis=1).astype(bf16)
    successor = jnp.concatenate([coords[1:], jnp.zeros((1, coords.shape[1]), f32)], axis=0).astype(bf16)
    weighted = rows * live[:, None].astype(bf16)
    dims = (((0,), (0,)), ((), ()))
    gram = lax.dot_general(weighted, rows, dims, preferred_element_type=f32) * weight_scale
    target = lax.dot_general(weighted, successor, dims, preferred_element_type=f32) * weight_scale
    return gram.astype(bf16), target.astype(bf16)


def on_device(snapshots, basis, lengths, owners):
    snap_count = snapshots.shape[1]
    devices = lax.axis_size("space")
    chips = devices // 2
    groups_tm = lax.axis_size("tm")
    own = lax.axis_index("space")
    parity = jnp.bitwise_and(own, 1)

    copies = jnp.broadcast_to(basis[None], (groups_tm,) + basis.shape)
    gathered = lax.all_to_all(copies, "tm", 0, 0, tiled=True).reshape(-1, basis.shape[1])
    target, live = plan(lengths[0], owners[0], own, parity, snap_count, chips)
    partial = lax.dot_general(snapshots, gathered, (((0,), (0,)), ((), ())), preferred_element_type=f32)

    swap = [(i, i ^ 1) for i in range(devices)]
    other = lax.ppermute(partial.astype(bf16), "space", swap)
    chip_sum = (partial + other.astype(f32)).astype(bf16)
    slot = lax.broadcasted_iota(jnp.int32, (chips * SLOTS, snap_count), 0)
    select = (slot == target[None, :]).astype(bf16)
    packed = jnp.dot(select, chip_sum, preferred_element_type=f32).astype(bf16)
    along_z = [[2 * z + c for z in range(chips)] for c in range(2)]
    parts = lax.all_to_all(
        packed.reshape(chips, SLOTS, -1), "space", 0, 0, axis_index_groups=along_z, tiled=True
    )
    coords = jnp.sum(parts.astype(f32), axis=0)
    gram, targets = library(coords, live, devices / snap_count)
    return gram[None, None], targets[None, None]


def solution(mesh):
    placed = (P("space", "tm"), P(("space", "tm"), None), P("tm", None), P("tm", None))
    return jax.shard_map(
        on_device,
        mesh=mesh,
        in_specs=placed,
        out_specs=(P("tm", "space", None, None), P("tm", "space", None, None)),
        check_vma=False,
    )
```

```python
import jax
import jax.numpy as jnp
import numpy as np
from jax import lax
from jax.sharding import PartitionSpec as P

QM = 16
SLOTS = 64
f32 = jnp.float32
bf16 = jnp.bfloat16


def plan(length, owner, own, parity, snap_count, chips):
    t = length.shape[0]
    ti = lax.broadcasted_iota(jnp.int32, (t, t), 0)
    tj = lax.broadcasted_iota(jnp.int32, (t, t), 1)
    before = tj < ti
    starts = jnp.sum(jnp.where(before, length[None, :], 0), axis=1)
    same = owner[:, None] == owner[None, :]
    offset = jnp.sum(jnp.where(before & same, length[None, :], 0), axis=1)
    chip = jnp.right_shift(owner, 1)
    other_parity = jnp.bitwise_and(chip + jnp.right_shift(own, 1), 1)
    place = other_parity * (chips // 2) + jnp.right_shift(chip, 1)
    base = jnp.where(
        jnp.bitwise_and(owner, 1) == parity,
        place * SLOTS + offset - starts,
        -2 * snap_count,
    )
    snap = lax.broadcasted_iota(jnp.int32, (t, snap_count), 1)
    member = (snap >= starts[:, None]) & (snap < (starts + length)[:, None])
    shift = jnp.sum(jnp.where(member, base[:, None], 0), axis=0)
    target = shift + jnp.arange(snap_count, dtype=jnp.int32)
    mine = owner == own
    total = jnp.sum(jnp.where(mine, length, 0))
    slot = lax.broadcasted_iota(jnp.int32, (SLOTS, t), 0)
    last = jnp.any(mine[None, :] & (slot == (offset + length - 1)[None, :]), axis=1)
    live = (jnp.arange(SLOTS) < total) & ~last
    return target, live


def library(coords, live, weight_scale):
    first_mode, second_mode = np.triu_indices(QM)
    pick_a = (first_mode[None, :] == lax.broadcasted_iota(jnp.int32, (QM, 1), 0)).astype(f32)
    pick_b = (second_mode[None, :] == lax.broadcasted_iota(jnp.int32, (QM, 1), 0)).astype(f32)
    lead = coords[:, :QM]
    hi = lax.Precision.HIGHEST
    products = jnp.dot(lead, pick_a, precision=hi) * jnp.dot(lead, pick_b, precision=hi)
    rows = jnp.concatenate([coords, products], axis=1).astype(bf16)
    successor = jnp.concatenate([coords[1:], jnp.zeros((1, coords.shape[1]), f32)], axis=0).astype(bf16)
    weighted = rows * live[:, None].astype(bf16)
    dims = (((0,), (0,)), ((), ()))
    gram = lax.dot_general(weighted, rows, dims, preferred_element_type=f32) * weight_scale
    target = lax.dot_general(weighted, successor, dims, preferred_element_type=f32) * weight_scale
    return gram.astype(bf16), target.astype(bf16)


def on_device(snapshots, basis, lengths, owners):
    snap_count = snapshots.shape[1]
    devices = lax.axis_size("space")
    chips = devices // 2
    groups_tm = lax.axis_size("tm")
    own = lax.axis_index("space")
    parity = jnp.bitwise_and(own, 1)

    copies = jnp.broadcast_to(basis[None], (groups_tm,) + basis.shape)
    gathered = lax.all_to_all(copies, "tm", 0, 0, tiled=True).reshape(-1, basis.shape[1])
    target, live = plan(lengths[0], owners[0], own, parity, snap_count, chips)
    swap = [(i, i ^ 1) for i in range(devices)]
    half = snap_count // 2
    sums = []
    for at in (0, half):
        partial = lax.dot_general(
            snapshots[:, at : at + half], gathered, (((0,), (0,)), ((), ())), preferred_element_type=f32
        )
        total = partial + lax.ppermute(partial, "space", swap)
        high = lax.reduce_precision(total, 8, 7)
        sums.append((high.astype(bf16), (total - high).astype(bf16)))
    slot = lax.broadcasted_iota(jnp.int32, (chips * SLOTS, snap_count), 0)
    select = (slot == target[None, :]).astype(bf16)
    dims = (((1,), (0,)), ((), ()))
    rows = chips // 2 * SLOTS
    keep, give = 0.0, 0.0
    for i, (high, low) in enumerate(sums):
        columns = select[:, i * half : (i + 1) * half]
        keep = keep + lax.dot_general(columns[:rows], high, dims, preferred_element_type=f32)
        keep = keep + lax.dot_general(columns[:rows], low, dims, preferred_element_type=f32)
        give = give + lax.dot_general(columns[rows:], high, dims, preferred_element_type=f32)
    give = give.astype(bf16)
    pair = {0: lambda z: z ^ 1, 1: lambda z: ((z + 1) ^ 1) - 1}
    pairs = [(2 * z + c, 2 * (pair[c](z) % chips) + c) for z in range(chips) for c in range(2)]
    summed = (keep + lax.ppermute(give, "space", pairs).astype(f32)).astype(bf16)
    along_z = [[2 * z + c for z in range(p, chips, 2)] for p in range(2) for c in range(2)]
    parts = lax.all_to_all(
        summed.reshape(chips // 2, SLOTS, -1), "space", 0, 0, axis_index_groups=along_z, tiled=True
    )
    coords = jnp.sum(parts.astype(f32), axis=0)
    gram, targets = library(coords, live, devices / snap_count)
    return gram[None, None], targets[None, None]


def solution(mesh):
    placed = (P("space", "tm"), P(("space", "tm"), None), P("tm", None), P("tm", None))
    return jax.shard_map(
        on_device,
        mesh=mesh,
        in_specs=placed,
        out_specs=(P("tm", "space", None, None), P("tm", "space", None, None)),
        check_vma=False,
    )
```

```python
import jax
import jax.numpy as jnp
import numpy as np
from jax import lax
from jax.experimental import pallas as pl
from jax.experimental.pallas import tpu as pltpu
from jax.sharding import PartitionSpec as P

QM = 16
SLOTS = 64
LANES = 128
f32 = jnp.float32
bf16 = jnp.bfloat16
i32 = jnp.int32
VMEM = pl.BlockSpec(memory_space=pltpu.VMEM)
SMEM = pl.BlockSpec(memory_space=pltpu.SMEM)


def iota(shape, axis):
    return lax.broadcasted_iota(i32, shape, axis)


def prepare_kernel(own_ref, length_ref, owner_ref, select_ref, live_ref):
    own = own_ref[0]
    t = length_ref.shape[1]
    snap_count = select_ref.shape[1]
    ti, tj = iota((t, t), 0), iota((t, t), 1)
    length_row = jnp.broadcast_to(length_ref[...], (t, t))
    owner_row = jnp.broadcast_to(owner_ref[...], (t, t))
    length_col = jnp.sum(jnp.where(ti == tj, length_row, 0), axis=1, keepdims=True)
    owner_col = jnp.sum(jnp.where(ti == tj, owner_row, 0), axis=1, keepdims=True)
    same = owner_row == owner_col
    starts = jnp.sum(jnp.where(tj < ti, length_row, 0), axis=1, keepdims=True)
    offset = jnp.sum(jnp.where((tj < ti) & same, length_row, 0), axis=1, keepdims=True)
    base = jnp.where(
        jnp.bitwise_and(owner_col, 1) == jnp.bitwise_and(own, 1),
        jnp.right_shift(owner_col, 1) * SLOTS + offset - starts,
        -2 * snap_count,
    )
    snap = iota((t, snap_count), 1)
    member = (snap >= starts) & (snap < starts + length_col)
    target = jnp.sum(jnp.where(member, base, 0), axis=0, keepdims=True) + iota((1, snap_count), 1)
    for at in range(0, select_ref.shape[0], SLOTS):
        slot = iota((SLOTS, snap_count), 0) + at
        select_ref[pl.ds(at, SLOTS), :] = jnp.where(slot == target, 1.0, 0.0).astype(bf16)
    row = slice(0, 1)
    offset_row = jnp.sum(jnp.where((ti < tj) & same, length_col, 0), axis=0, keepdims=True)
    mine = owner_row[row] == own
    total = jnp.sum(jnp.where(mine, length_row[row], 0), axis=1, keepdims=True)
    here = iota((SLOTS, t), 0)
    ends = mine & (here == offset_row + length_row[row] - 1)
    last = jnp.sum(jnp.where(ends, 1, 0), axis=1, keepdims=True)
    live = (iota((SLOTS, 1), 0) < total) & (last == 0)
    live_ref[...] = jnp.broadcast_to(jnp.where(live, 1.0, 0.0), (SLOTS, LANES))


def spread_kernel(basis_ref, copies_ref, done):
    count = copies_ref.shape[0]
    moves = [pltpu.make_async_copy(basis_ref, copies_ref.at[i], done.at[i]) for i in range(count)]
    for move in moves:
        move.start()
    for move in moves:
        move.wait()


def spread(basis, count):
    return pl.pallas_call(
        spread_kernel,
        out_shape=jax.ShapeDtypeStruct((count,) + basis.shape, basis.dtype),
        in_specs=[VMEM],
        out_specs=pl.BlockSpec(memory_space=pl.ANY),
        scratch_shapes=[pltpu.SemaphoreType.DMA((count,))],
        name="spread",
    )(basis)


def project_kernel(snapshots_ref, basis_ref, partial_ref, sent_ref):
    piece = lax.dot_general(
        basis_ref[...], snapshots_ref[...], (((0,), (0,)), ((), ())), preferred_element_type=f32
    )
    partial_ref[...] = piece
    sent_ref[...] = piece.astype(bf16)


def project(snapshots, basis, step):
    cells, snap_count = snapshots.shape
    modes = basis.shape[1]
    piece = pl.BlockSpec((modes, step), lambda i: (0, i))
    return pl.pallas_call(
        project_kernel,
        grid=(snap_count // step,),
        out_shape=tuple(jax.ShapeDtypeStruct((modes, snap_count), kind) for kind in (f32, bf16)),
        in_specs=[pl.BlockSpec((cells, step), lambda i: (0, i)), VMEM],
        out_specs=(piece, piece),
        compiler_params=pltpu.CompilerParams(vmem_limit_bytes=50 << 20),
        cost_estimate=pl.CostEstimate(
            flops=2 * cells * snap_count * modes, bytes_accessed=2 * cells * snap_count, transcendentals=0
        ),
        name="project",
    )(snapshots, basis)


def pack_kernel(select_ref, partial_ref, other_ref, packed_ref):
    chip_sum = (partial_ref[...] + other_ref[...].astype(f32)).astype(bf16)
    step = 256
    for at in range(0, select_ref.shape[0], step):
        packed_ref[pl.ds(at, step), :] = lax.dot_general(
            select_ref[pl.ds(at, step), :], chip_sum, (((1,), (1,)), ((), ())), preferred_element_type=f32
        ).astype(bf16)


def library_kernel(weight_scale, parts_ref, live_ref, pick_ref, gram_ref, target_ref):
    coords = jnp.sum(parts_ref[...].astype(f32), axis=0)
    modes = coords.shape[1]
    terms = pick_ref.shape[1] // 2
    both = jnp.dot(
        coords[:, :LANES], pick_ref[...], precision=lax.Precision.HIGHEST, preferred_element_type=f32
    )
    products = both[:, :terms] * both[:, terms:]
    theta = jnp.concatenate([coords, products], axis=1).astype(bf16)[:, : gram_ref.shape[0]]
    live = live_ref[:, :1].astype(bf16)
    weighted = theta * live
    row = iota((SLOTS, modes), 0)
    successor = jnp.where(row < SLOTS - 1, pltpu.roll(coords, SLOTS - 1, 0), 0.0).astype(bf16)
    dims = (((0,), (0,)), ((), ()))
    gram = lax.dot_general(weighted, theta, dims, preferred_element_type=f32) * weight_scale
    gram_ref[...] = gram.astype(bf16)
    target = lax.dot_general(weighted, successor, dims, preferred_element_type=f32) * weight_scale
    target_ref[...] = target.astype(bf16)


def call(kernel, name, outs, specs, flops, nbytes, mib=24, **more):
    return pl.pallas_call(
        kernel,
        out_shape=outs,
        in_specs=specs,
        out_specs=jax.tree.map(lambda _: VMEM, outs),
        compiler_params=pltpu.CompilerParams(vmem_limit_bytes=mib << 20),
        cost_estimate=pl.CostEstimate(flops=flops, bytes_accessed=nbytes, transcendentals=0),
        name=name,
        **more,
    )


def picks():
    first_mode, second_mode = np.triu_indices(QM)
    table = np.zeros((LANES, 4 * LANES), np.float32)
    for term, (a, b) in enumerate(zip(first_mode, second_mode)):
        table[a, term] = 1.0
        table[b, 2 * LANES + term] = 1.0
    return len(first_mode), table


def on_device(snapshots, basis, lengths, owners):
    cells, snap_count = snapshots.shape
    modes = basis.shape[1]
    devices = lax.axis_size("space")
    chips = devices // 2
    groups_tm = lax.axis_size("tm")
    own = lax.axis_index("space")
    rows = chips * SLOTS
    shape = jax.ShapeDtypeStruct

    gathered = lax.all_to_all(spread(basis, groups_tm), "tm", 0, 0, tiled=True).reshape(-1, modes)
    select, live = call(
        prepare_kernel,
        "prepare",
        (shape((rows, snap_count), bf16), shape((SLOTS, LANES), f32)),
        [SMEM, VMEM, VMEM],
        4 * rows * snap_count,
        2 * rows * snap_count,
    )(own.reshape(1), lengths, owners)
    gathered, select = lax.optimization_barrier((gathered, select))
    partial, sent = project(snapshots, gathered, 256)
    swap = [(i, i ^ 1) for i in range(devices)]
    other = lax.ppermute(sent, "space", swap)
    packed = call(
        pack_kernel,
        "pack",
        shape((rows, modes), bf16),
        [VMEM, VMEM, VMEM],
        2 * rows * snap_count * modes,
        6 * snap_count * modes,
    )(select, partial, other)
    along_z = [[2 * z + c for z in range(chips)] for c in range(2)]
    parts = lax.all_to_all(
        packed.reshape(chips, SLOTS, -1), "space", 0, 0, axis_index_groups=along_z, tiled=True
    )
    term_count, table = picks()
    terms = modes + term_count
    gram, target = call(
        lambda *refs: library_kernel(devices / snap_count, *refs),
        "library",
        (shape((terms, terms), bf16), shape((terms, modes), bf16)),
        [VMEM, VMEM, VMEM],
        2 * SLOTS * terms * (terms + modes),
        2 * terms * (terms + modes),
    )(parts, live, jnp.asarray(table))
    return gram[None, None], target[None, None]


def solution(mesh):
    placed = (P("space", "tm"), P(("space", "tm"), None), P("tm", None), P("tm", None))
    return jax.shard_map(
        on_device,
        mesh=mesh,
        in_specs=placed,
        out_specs=(P("tm", "space", None, None), P("tm", "space", None, None)),
        check_vma=False,
    )
```

```python
import jax
import jax.numpy as jnp
import numpy as np
from jax import lax
from jax.experimental import pallas as pl
from jax.experimental.pallas import tpu as pltpu
from jax.sharding import PartitionSpec as P

QM = 16
SLOTS = 64
LANES = 128
f32 = jnp.float32
bf16 = jnp.bfloat16
i32 = jnp.int32
VMEM = pl.BlockSpec(memory_space=pltpu.VMEM)
SMEM = pl.BlockSpec(memory_space=pltpu.SMEM)


def iota(shape, axis):
    return lax.broadcasted_iota(i32, shape, axis)


def prepare_kernel(own_ref, length_ref, owner_ref, select_ref, live_ref):
    own = own_ref[0]
    t = length_ref.shape[1]
    snap_count = select_ref.shape[1]
    ti, tj = iota((t, t), 0), iota((t, t), 1)
    length_row = jnp.broadcast_to(length_ref[...], (t, t))
    owner_row = jnp.broadcast_to(owner_ref[...], (t, t))
    length_col = jnp.sum(jnp.where(ti == tj, length_row, 0), axis=1, keepdims=True)
    owner_col = jnp.sum(jnp.where(ti == tj, owner_row, 0), axis=1, keepdims=True)
    same = owner_row == owner_col
    starts = jnp.sum(jnp.where(tj < ti, length_row, 0), axis=1, keepdims=True)
    offset = jnp.sum(jnp.where((tj < ti) & same, length_row, 0), axis=1, keepdims=True)
    base = jnp.where(
        jnp.bitwise_and(owner_col, 1) == jnp.bitwise_and(own, 1),
        jnp.right_shift(owner_col, 1) * SLOTS + offset - starts,
        -2 * snap_count,
    )
    snap = iota((t, snap_count), 1)
    member = (snap >= starts) & (snap < starts + length_col)
    target = jnp.sum(jnp.where(member, base, 0), axis=0, keepdims=True) + iota((1, snap_count), 1)
    for at in range(0, select_ref.shape[0], SLOTS):
        slot = iota((SLOTS, snap_count), 0) + at
        select_ref[pl.ds(at, SLOTS), :] = jnp.where(slot == target, 1.0, 0.0).astype(bf16)
    row = slice(0, 1)
    offset_row = jnp.sum(jnp.where((ti < tj) & same, length_col, 0), axis=0, keepdims=True)
    mine = owner_row[row] == own
    total = jnp.sum(jnp.where(mine, length_row[row], 0), axis=1, keepdims=True)
    here = iota((SLOTS, t), 0)
    ends = mine & (here == offset_row + length_row[row] - 1)
    last = jnp.sum(jnp.where(ends, 1, 0), axis=1, keepdims=True)
    live = (iota((SLOTS, 1), 0) < total) & (last == 0)
    live_ref[...] = jnp.broadcast_to(jnp.where(live, 1.0, 0.0), (SLOTS, LANES))


def project_kernel(snapshots_ref, basis_ref, partial_ref, sent_ref):
    left = jnp.concatenate([basis_ref[i] for i in range(basis_ref.shape[0])], axis=1)
    piece = jnp.dot(left, snapshots_ref[...], preferred_element_type=f32)
    step = pl.program_id(0)

    @pl.when(step == 0)
    def _():
        partial_ref[...] = piece

    @pl.when(step > 0)
    def _():
        total = partial_ref[...] + piece
        partial_ref[...] = total
        sent_ref[...] = total.astype(bf16)


def project(snapshots, basis, steps):
    cells, snap_count = snapshots.shape
    blocks, modes, width = basis.shape
    whole = pl.BlockSpec((modes, snap_count), lambda i: (0, 0))
    return pl.pallas_call(
        project_kernel,
        grid=(steps,),
        out_shape=tuple(jax.ShapeDtypeStruct((modes, snap_count), kind) for kind in (f32, bf16)),
        in_specs=[
            pl.BlockSpec((cells // steps, snap_count), lambda i: (i, 0)),
            pl.BlockSpec((blocks // steps, modes, width), lambda i: (i, 0, 0)),
        ],
        out_specs=(whole, whole),
        compiler_params=pltpu.CompilerParams(vmem_limit_bytes=50 << 20),
        cost_estimate=pl.CostEstimate(
            flops=2 * cells * snap_count * modes, bytes_accessed=2 * cells * snap_count, transcendentals=0
        ),
        name="project",
    )(snapshots, basis)


def pack_kernel(select_ref, partial_ref, other_ref, packed_ref):
    chip_sum = (partial_ref[...] + other_ref[...].astype(f32)).astype(bf16)
    step = 256
    for at in range(0, select_ref.shape[0], step):
        packed_ref[pl.ds(at, step), :] = lax.dot_general(
            select_ref[pl.ds(at, step), :], chip_sum, (((1,), (1,)), ((), ())), preferred_element_type=f32
        ).astype(bf16)


def library_kernel(weight_scale, parts_ref, live_ref, pick_ref, gram_ref, target_ref):
    coords = jnp.sum(parts_ref[...].astype(f32), axis=0)
    modes = coords.shape[1]
    terms = pick_ref.shape[1] // 2
    both = jnp.dot(
        coords[:, :LANES], pick_ref[...], precision=lax.Precision.HIGHEST, preferred_element_type=f32
    )
    products = both[:, :terms] * both[:, terms:]
    theta = jnp.concatenate([coords, products], axis=1).astype(bf16)[:, : gram_ref.shape[0]]
    live = live_ref[:, :1].astype(bf16)
    weighted = theta * live
    row = iota((SLOTS, modes), 0)
    successor = jnp.where(row < SLOTS - 1, pltpu.roll(coords, SLOTS - 1, 0), 0.0).astype(bf16)
    dims = (((0,), (0,)), ((), ()))
    gram = lax.dot_general(weighted, theta, dims, preferred_element_type=f32) * weight_scale
    gram_ref[...] = gram.astype(bf16)
    target = lax.dot_general(weighted, successor, dims, preferred_element_type=f32) * weight_scale
    target_ref[...] = target.astype(bf16)


def call(kernel, name, outs, specs, flops, nbytes, mib=24, **more):
    return pl.pallas_call(
        kernel,
        out_shape=outs,
        in_specs=specs,
        out_specs=jax.tree.map(lambda _: VMEM, outs),
        compiler_params=pltpu.CompilerParams(vmem_limit_bytes=mib << 20),
        cost_estimate=pl.CostEstimate(flops=flops, bytes_accessed=nbytes, transcendentals=0),
        name=name,
        **more,
    )


def picks():
    first_mode, second_mode = np.triu_indices(QM)
    table = np.zeros((LANES, 4 * LANES), np.float32)
    for term, (a, b) in enumerate(zip(first_mode, second_mode)):
        table[a, term] = 1.0
        table[b, 2 * LANES + term] = 1.0
    return len(first_mode), table


def on_device(snapshots, basis, lengths, owners):
    cells, snap_count = snapshots.shape
    modes = basis.shape[1]
    devices = lax.axis_size("space")
    chips = devices // 2
    groups_tm = lax.axis_size("tm")
    own = lax.axis_index("space")
    rows = chips * SLOTS
    shape = jax.ShapeDtypeStruct

    copies = jnp.broadcast_to(basis.T[None], (groups_tm, modes, basis.shape[0]))
    gathered = lax.all_to_all(copies, "tm", 0, 0, tiled=True)
    select, live = call(
        prepare_kernel,
        "prepare",
        (shape((rows, snap_count), bf16), shape((SLOTS, LANES), f32)),
        [SMEM, VMEM, VMEM],
        4 * rows * snap_count,
        2 * rows * snap_count,
    )(own.reshape(1), lengths, owners)
    partial, sent = project(snapshots, gathered, 2)
    swap = [(i, i ^ 1) for i in range(devices)]
    other = lax.ppermute(sent, "space", swap)
    packed = call(
        pack_kernel,
        "pack",
        shape((rows, modes), bf16),
        [VMEM, VMEM, VMEM],
        2 * rows * snap_count * modes,
        6 * snap_count * modes,
    )(select, partial, other)
    along_z = [[2 * z + c for z in range(chips)] for c in range(2)]
    parts = lax.all_to_all(
        packed.reshape(chips, SLOTS, -1), "space", 0, 0, axis_index_groups=along_z, tiled=True
    )
    term_count, table = picks()
    terms = modes + term_count
    gram, target = call(
        lambda *refs: library_kernel(devices / snap_count, *refs),
        "library",
        (shape((terms, terms), bf16), shape((terms, modes), bf16)),
        [VMEM, VMEM, VMEM],
        2 * SLOTS * terms * (terms + modes),
        2 * terms * (terms + modes),
    )(parts, live, jnp.asarray(table))
    return gram[None, None], target[None, None]


def solution(mesh):
    placed = (P("space", "tm"), P(("space", "tm"), None), P("tm", None), P("tm", None))
    return jax.shard_map(
        on_device,
        mesh=mesh,
        in_specs=placed,
        out_specs=(P("tm", "space", None, None), P("tm", "space", None, None)),
        check_vma=False,
    )
```

```python
import jax
import jax.numpy as jnp
import numpy as np
from jax import lax
from jax.experimental import pallas as pl
from jax.experimental.pallas import tpu as pltpu
from jax.sharding import PartitionSpec as P

QM = 16
SLOTS = 64
LANES = 128
FIRST_PAIR = 4
FIRST_TM = 10
f32 = jnp.float32
bf16 = jnp.bfloat16
i32 = jnp.int32
VMEM = pl.BlockSpec(memory_space=pltpu.VMEM)
SMEM = pl.BlockSpec(memory_space=pltpu.SMEM)


def rotated(pair, count):
    return jnp.bitwise_and(pair - FIRST_PAIR, count - 1)


def iota(shape, axis):
    return lax.broadcasted_iota(i32, shape, axis)


def prepare_kernel(own_ref, length_ref, owner_ref, select_ref, live_ref):
    own = own_ref[0]
    t = length_ref.shape[1]
    snap_count = select_ref.shape[1]
    ti, tj = iota((t, t), 0), iota((t, t), 1)
    length_row = jnp.broadcast_to(length_ref[...], (t, t))
    owner_row = jnp.broadcast_to(owner_ref[...], (t, t))
    length_col = jnp.sum(jnp.where(ti == tj, length_row, 0), axis=1, keepdims=True)
    owner_col = jnp.sum(jnp.where(ti == tj, owner_row, 0), axis=1, keepdims=True)
    same = owner_row == owner_col
    starts = jnp.sum(jnp.where(tj < ti, length_row, 0), axis=1, keepdims=True)
    offset = jnp.sum(jnp.where((tj < ti) & same, length_row, 0), axis=1, keepdims=True)
    chip = jnp.right_shift(owner_col, 1)
    across = jnp.bitwise_and(chip + jnp.right_shift(own, 1), 1)
    half = select_ref.shape[0] // (2 * SLOTS)
    place = across * half + rotated(jnp.right_shift(chip, 1), half)
    base = jnp.where(
        jnp.bitwise_and(owner_col, 1) == jnp.bitwise_and(own, 1),
        place * SLOTS + offset - starts,
        -2 * snap_count,
    )
    snap = iota((t, snap_count), 1)
    member = (snap >= starts) & (snap < starts + length_col)
    target = jnp.sum(jnp.where(member, base, 0), axis=0, keepdims=True) + iota((1, snap_count), 1)
    for at in range(0, select_ref.shape[0], SLOTS):
        slot = iota((SLOTS, snap_count), 0) + at
        select_ref[pl.ds(at, SLOTS), :] = jnp.where(slot == target, 1.0, 0.0).astype(bf16)
    row = slice(0, 1)
    offset_row = jnp.sum(jnp.where((ti < tj) & same, length_col, 0), axis=0, keepdims=True)
    mine = owner_row[row] == own
    total = jnp.sum(jnp.where(mine, length_row[row], 0), axis=1, keepdims=True)
    here = iota((SLOTS, t), 0)
    ends = mine & (here == offset_row + length_row[row] - 1)
    last = jnp.sum(jnp.where(ends, 1, 0), axis=1, keepdims=True)
    live = (iota((SLOTS, 1), 0) < total) & (last == 0)
    live_ref[...] = jnp.broadcast_to(jnp.where(live, 1.0, 0.0), (SLOTS, LANES))


def project_kernel(snapshots_ref, basis_ref, partial_ref, sent_ref):
    step = pl.program_id(0)
    blocks, _, width = basis_ref.shape
    count = snapshots_ref.shape[0] // width
    turn = [jnp.bitwise_and(step * count + i - FIRST_TM, blocks - 1) for i in range(count)]
    left = jnp.concatenate([basis_ref[i] for i in turn], axis=1)
    piece = jnp.dot(left, snapshots_ref[...], preferred_element_type=f32)

    @pl.when(step == 0)
    def _():
        partial_ref[...] = piece

    @pl.when(step > 0)
    def _():
        total = partial_ref[...] + piece
        partial_ref[...] = total
        high = total.astype(bf16)
        sent_ref[: total.shape[0], :] = high
        sent_ref[total.shape[0] :, :] = (total[:QM] - high[:QM].astype(f32)).astype(bf16)


def project(snapshots, basis, steps):
    cells, snap_count = snapshots.shape
    modes = basis.shape[1]
    heights = (modes, modes + QM)
    return pl.pallas_call(
        project_kernel,
        grid=(steps,),
        out_shape=tuple(jax.ShapeDtypeStruct((h, snap_count), kind) for h, kind in zip(heights, (f32, bf16))),
        in_specs=[
            pl.BlockSpec((cells // steps, snap_count), lambda i: (i, 0)),
            VMEM,
        ],
        out_specs=tuple(pl.BlockSpec((h, snap_count), lambda i: (0, 0)) for h in heights),
        compiler_params=pltpu.CompilerParams(vmem_limit_bytes=50 << 20),
        cost_estimate=pl.CostEstimate(
            flops=2 * cells * snap_count * modes, bytes_accessed=2 * cells * snap_count, transcendentals=0
        ),
        name="project",
    )(snapshots, basis)


NT = (((1,), (1,)), ((), ()))


def chip_sum(partial_ref, other_ref):
    modes = partial_ref.shape[0]
    total = partial_ref[...] + other_ref[:modes].astype(f32)
    lead = total[:QM] + other_ref[modes:].astype(f32)
    total = jnp.concatenate([lead, total[QM:]], axis=0)
    high = total.astype(bf16)
    return high, (total - high.astype(f32)).astype(bf16)


def give_kernel(select_ref, partial_ref, other_ref, given_ref):
    high, _ = chip_sum(partial_ref, other_ref)
    count = given_ref.shape[0]
    given_ref[...] = lax.dot_general(
        select_ref[count:, :], high, NT, preferred_element_type=f32
    ).astype(bf16)


def keep_kernel(select_ref, partial_ref, other_ref, kept_ref):
    high, low = chip_sum(partial_ref, other_ref)
    select = select_ref[: kept_ref.shape[0], :]
    kept_ref[...] = lax.dot_general(select, high, NT, preferred_element_type=f32) + lax.dot_general(
        select, low, NT, preferred_element_type=f32
    )


def merge_kernel(own_ref, kept_ref, given_ref, merged_ref, mine_ref):
    merged_ref[...] = (kept_ref[...] + given_ref[...].astype(f32)).astype(bf16)
    me = rotated(jnp.right_shift(own_ref[0], 2), kept_ref.shape[0] // SLOTS)
    at = pl.ds(pl.multiple_of(me * SLOTS, SLOTS), SLOTS)
    mine_ref[...] = kept_ref[at, :] + given_ref[at, :].astype(f32)


def library_kernel(weight_scale, own_ref, parts_ref, mine_ref, live_ref, pick_ref, gram_ref, target_ref):
    me = rotated(jnp.right_shift(own_ref[0], 2), parts_ref.shape[0])
    coords = mine_ref[...]
    for i in range(parts_ref.shape[0]):
        coords = coords + jnp.where(i == me, 0.0, parts_ref[i].astype(f32))
    modes = coords.shape[1]
    terms = pick_ref.shape[1] // 2
    both = jnp.dot(
        coords[:, :LANES], pick_ref[...], precision=lax.Precision.HIGHEST, preferred_element_type=f32
    )
    products = both[:, :terms] * both[:, terms:]
    theta = jnp.concatenate([coords, products], axis=1).astype(bf16)[:, : gram_ref.shape[0]]
    live = live_ref[:, :1].astype(bf16)
    weighted = theta * live
    row = iota((SLOTS, modes), 0)
    successor = jnp.where(row < SLOTS - 1, pltpu.roll(coords, SLOTS - 1, 0), 0.0).astype(bf16)
    dims = (((0,), (0,)), ((), ()))
    gram = lax.dot_general(weighted, theta, dims, preferred_element_type=f32) * weight_scale
    gram_ref[...] = gram.astype(bf16)
    target = lax.dot_general(weighted, successor, dims, preferred_element_type=f32) * weight_scale
    target_ref[...] = target.astype(bf16)


def call(kernel, name, outs, specs, flops, nbytes, mib=24, **more):
    return pl.pallas_call(
        kernel,
        out_shape=outs,
        in_specs=specs,
        out_specs=jax.tree.map(lambda _: VMEM, outs),
        compiler_params=pltpu.CompilerParams(vmem_limit_bytes=mib << 20),
        cost_estimate=pl.CostEstimate(flops=flops, bytes_accessed=nbytes, transcendentals=0),
        name=name,
        **more,
    )


def picks():
    first_mode, second_mode = np.triu_indices(QM)
    table = np.zeros((LANES, 4 * LANES), np.float32)
    for term, (a, b) in enumerate(zip(first_mode, second_mode)):
        table[a, term] = 1.0
        table[b, 2 * LANES + term] = 1.0
    return len(first_mode), table


def on_device(snapshots, basis, lengths, owners):
    cells, snap_count = snapshots.shape
    modes = basis.shape[1]
    devices = lax.axis_size("space")
    chips = devices // 2
    groups_tm = lax.axis_size("tm")
    own = lax.axis_index("space")
    rows = chips * SLOTS
    shape = jax.ShapeDtypeStruct

    copies = jnp.broadcast_to(basis.T[None], (groups_tm, modes, basis.shape[0]))
    order = [(i + FIRST_TM) % groups_tm for i in range(groups_tm)]
    gathered = lax.all_to_all(copies, "tm", 0, 0, axis_index_groups=[order], tiled=True)
    select, live = call(
        prepare_kernel,
        "prepare",
        (shape((rows, snap_count), bf16), shape((SLOTS, LANES), f32)),
        [SMEM, VMEM, VMEM],
        4 * rows * snap_count,
        2 * rows * snap_count,
    )(own.reshape(1), lengths, owners)
    partial, sent = project(snapshots, gathered, 2)
    swap = [(i, i ^ 1) for i in range(devices)]
    other = lax.ppermute(sent, "space", swap)
    kept_rows = rows // 2
    flops = rows * snap_count * modes
    given = call(
        give_kernel, "give", shape((kept_rows, modes), bf16), [VMEM] * 3, flops, 4 * rows * modes
    )(select, partial, other)
    near = [(2 * z, 2 * (z ^ 1)) for z in range(chips)]
    near += [(2 * z + 1, 2 * ((((z + 1) ^ 1) - 1) % chips) + 1) for z in range(chips)]
    given = lax.ppermute(given, "space", near)
    kept = call(
        keep_kernel, "keep", shape((kept_rows, modes), f32), [VMEM] * 3, 2 * flops, 4 * rows * modes
    )(select, partial, other)
    merged, mine = call(
        merge_kernel,
        "merge",
        (shape((kept_rows, modes), bf16), shape((SLOTS, modes), f32)),
        [SMEM, VMEM, VMEM],
        rows * modes,
        4 * rows * modes,
    )(own.reshape(1), kept, given)
    pairs = chips // 2
    order = [(i + FIRST_PAIR) % pairs for i in range(pairs)]
    along_z = [[2 * (2 * pair + p) + c for pair in order] for p in range(2) for c in range(2)]
    parts = lax.all_to_all(
        merged.reshape(pairs, SLOTS, -1), "space", 0, 0, axis_index_groups=along_z, tiled=True
    )
    term_count, table = picks()
    terms = modes + term_count
    gram, target = call(
        lambda *refs: library_kernel(devices / snap_count, *refs),
        "library",
        (shape((terms, terms), bf16), shape((terms, modes), bf16)),
        [SMEM] + [VMEM] * 4,
        2 * SLOTS * terms * (terms + modes),
        2 * terms * (terms + modes),
    )(own.reshape(1), parts, mine, live, jnp.asarray(table))
    return gram[None, None], target[None, None]


def solution(mesh):
    placed = (P("space", "tm"), P(("space", "tm"), None), P("tm", None), P("tm", None))
    return jax.shard_map(
        on_device,
        mesh=mesh,
        in_specs=placed,
        out_specs=(P("tm", "space", None, None), P("tm", "space", None, None)),
        check_vma=False,
    )
```

```python
import jax
import jax.numpy as jnp
import numpy as np
from jax import lax
from jax.experimental import pallas as pl
from jax.experimental.pallas import tpu as pltpu
from jax.sharding import PartitionSpec as P

QM = 16
SLOTS = 64
LANES = 128
FIRST_PAIR = 4
FIRST_TM = 10
f32 = jnp.float32
bf16 = jnp.bfloat16
i32 = jnp.int32
VMEM = pl.BlockSpec(memory_space=pltpu.VMEM)
SMEM = pl.BlockSpec(memory_space=pltpu.SMEM)


def rotated(pair, count):
    return jnp.bitwise_and(pair - FIRST_PAIR, count - 1)


def iota(shape, axis):
    return lax.broadcasted_iota(i32, shape, axis)


def prepare_kernel(own_ref, length_ref, owner_ref, select_ref, live_ref):
    own = own_ref[0]
    t = length_ref.shape[1]
    snap_count = select_ref.shape[1]
    ti, tj = iota((t, t), 0), iota((t, t), 1)
    length_row = jnp.broadcast_to(length_ref[...], (t, t))
    owner_row = jnp.broadcast_to(owner_ref[...], (t, t))
    length_col = jnp.sum(jnp.where(ti == tj, length_row, 0), axis=1, keepdims=True)
    owner_col = jnp.sum(jnp.where(ti == tj, owner_row, 0), axis=1, keepdims=True)
    same = owner_row == owner_col
    starts = jnp.sum(jnp.where(tj < ti, length_row, 0), axis=1, keepdims=True)
    offset = jnp.sum(jnp.where((tj < ti) & same, length_row, 0), axis=1, keepdims=True)
    chip = jnp.right_shift(owner_col, 1)
    across = jnp.bitwise_and(chip + jnp.right_shift(own, 1), 1)
    half = select_ref.shape[0] // (2 * SLOTS)
    place = across * half + rotated(jnp.right_shift(chip, 1), half)
    base = jnp.where(
        jnp.bitwise_and(owner_col, 1) == jnp.bitwise_and(own, 1),
        place * SLOTS + offset - starts,
        -2 * snap_count,
    )
    snap = iota((t, snap_count), 1)
    member = (snap >= starts) & (snap < starts + length_col)
    target = jnp.sum(jnp.where(member, base, 0), axis=0, keepdims=True) + iota((1, snap_count), 1)
    for at in range(0, select_ref.shape[0], SLOTS):
        slot = iota((SLOTS, snap_count), 0) + at
        select_ref[pl.ds(at, SLOTS), :] = jnp.where(slot == target, 1.0, 0.0).astype(bf16)
    row = slice(0, 1)
    offset_row = jnp.sum(jnp.where((ti < tj) & same, length_col, 0), axis=0, keepdims=True)
    mine = owner_row[row] == own
    total = jnp.sum(jnp.where(mine, length_row[row], 0), axis=1, keepdims=True)
    here = iota((SLOTS, t), 0)
    ends = mine & (here == offset_row + length_row[row] - 1)
    last = jnp.sum(jnp.where(ends, 1, 0), axis=1, keepdims=True)
    live = (iota((SLOTS, 1), 0) < total) & (last == 0)
    live_ref[...] = jnp.broadcast_to(jnp.where(live, 1.0, 0.0), (SLOTS, LANES))


def project_kernel(snapshots_ref, basis_ref, partial_ref, sent_ref):
    step = pl.program_id(0)
    blocks, width, modes = basis_ref.shape
    count = snapshots_ref.shape[0] // width
    turn = [jnp.bitwise_and(step * count + i - FIRST_TM, blocks - 1) for i in range(count)]
    basis = jnp.concatenate([basis_ref[i] for i in turn], axis=0)
    piece = lax.dot_general(
        basis, snapshots_ref[...], (((0,), (0,)), ((), ())), preferred_element_type=f32
    )

    @pl.when(step == 0)
    def _():
        partial_ref[...] = piece

    @pl.when(step > 0)
    def _():
        total = partial_ref[...] + piece
        partial_ref[...] = total
        high = total.astype(bf16)
        sent_ref[: total.shape[0], :] = high
        sent_ref[total.shape[0] :, :] = (total[:QM] - high[:QM].astype(f32)).astype(bf16)


def project(snapshots, basis, steps):
    cells, snap_count = snapshots.shape
    modes = basis.shape[2]
    heights = (modes, modes + QM)
    return pl.pallas_call(
        project_kernel,
        grid=(steps,),
        out_shape=tuple(jax.ShapeDtypeStruct((h, snap_count), kind) for h, kind in zip(heights, (f32, bf16))),
        in_specs=[
            pl.BlockSpec((cells // steps, snap_count), lambda i: (i, 0)),
            VMEM,
        ],
        out_specs=tuple(pl.BlockSpec((h, snap_count), lambda i: (0, 0)) for h in heights),
        compiler_params=pltpu.CompilerParams(vmem_limit_bytes=50 << 20),
        cost_estimate=pl.CostEstimate(
            flops=2 * cells * snap_count * modes, bytes_accessed=2 * cells * snap_count, transcendentals=0
        ),
        name="project",
    )(snapshots, basis)


NT = (((1,), (1,)), ((), ()))


def chip_sum(partial_ref, other_ref):
    modes = partial_ref.shape[0]
    total = partial_ref[...] + other_ref[:modes].astype(f32)
    lead = total[:QM] + other_ref[modes:].astype(f32)
    total = jnp.concatenate([lead, total[QM:]], axis=0)
    high = total.astype(bf16)
    return high, (total - high.astype(f32)).astype(bf16)


def give_kernel(select_ref, partial_ref, other_ref, given_ref):
    high, _ = chip_sum(partial_ref, other_ref)
    count = given_ref.shape[0]
    given_ref[...] = lax.dot_general(
        select_ref[count:, :], high, NT, preferred_element_type=f32
    ).astype(bf16)


def keep_kernel(select_ref, partial_ref, other_ref, kept_ref):
    high, low = chip_sum(partial_ref, other_ref)
    select = select_ref[: kept_ref.shape[0], :]
    kept_ref[...] = lax.dot_general(select, high, NT, preferred_element_type=f32) + lax.dot_general(
        select, low, NT, preferred_element_type=f32
    )


def merge_kernel(own_ref, kept_ref, given_ref, merged_ref, mine_ref):
    merged_ref[...] = (kept_ref[...] + given_ref[...].astype(f32)).astype(bf16)
    me = rotated(jnp.right_shift(own_ref[0], 2), kept_ref.shape[0] // SLOTS)
    at = pl.ds(pl.multiple_of(me * SLOTS, SLOTS), SLOTS)
    mine_ref[...] = kept_ref[at, :] + given_ref[at, :].astype(f32)


def library_kernel(weight_scale, own_ref, parts_ref, mine_ref, live_ref, pick_ref, gram_ref, target_ref):
    me = rotated(jnp.right_shift(own_ref[0], 2), parts_ref.shape[0])
    coords = mine_ref[...]
    for i in range(parts_ref.shape[0]):
        coords = coords + jnp.where(i == me, 0.0, parts_ref[i].astype(f32))
    modes = coords.shape[1]
    terms = pick_ref.shape[1] // 2
    both = jnp.dot(
        coords[:, :LANES], pick_ref[...], precision=lax.Precision.HIGHEST, preferred_element_type=f32
    )
    products = both[:, :terms] * both[:, terms:]
    theta = jnp.concatenate([coords, products], axis=1).astype(bf16)[:, : gram_ref.shape[0]]
    live = live_ref[:, :1].astype(bf16)
    weighted = theta * live
    row = iota((SLOTS, modes), 0)
    successor = jnp.where(row < SLOTS - 1, pltpu.roll(coords, SLOTS - 1, 0), 0.0).astype(bf16)
    dims = (((0,), (0,)), ((), ()))
    gram = lax.dot_general(weighted, theta, dims, preferred_element_type=f32) * weight_scale
    gram_ref[...] = gram.astype(bf16)
    target = lax.dot_general(weighted, successor, dims, preferred_element_type=f32) * weight_scale
    target_ref[...] = target.astype(bf16)


def call(kernel, name, outs, specs, flops, nbytes, mib=24, **more):
    return pl.pallas_call(
        kernel,
        out_shape=outs,
        in_specs=specs,
        out_specs=jax.tree.map(lambda _: VMEM, outs),
        compiler_params=pltpu.CompilerParams(vmem_limit_bytes=mib << 20),
        cost_estimate=pl.CostEstimate(flops=flops, bytes_accessed=nbytes, transcendentals=0),
        name=name,
        **more,
    )


def picks():
    first_mode, second_mode = np.triu_indices(QM)
    table = np.zeros((LANES, 4 * LANES), np.float32)
    for term, (a, b) in enumerate(zip(first_mode, second_mode)):
        table[a, term] = 1.0
        table[b, 2 * LANES + term] = 1.0
    return len(first_mode), table


def on_device(snapshots, basis, lengths, owners):
    cells, snap_count = snapshots.shape
    modes = basis.shape[1]
    devices = lax.axis_size("space")
    chips = devices // 2
    groups_tm = lax.axis_size("tm")
    own = lax.axis_index("space")
    rows = chips * SLOTS
    shape = jax.ShapeDtypeStruct

    copies = jnp.broadcast_to(basis[None], (groups_tm,) + basis.shape)
    order = [(i + FIRST_TM) % groups_tm for i in range(groups_tm)]
    gathered = lax.all_to_all(copies, "tm", 0, 0, axis_index_groups=[order], tiled=True)
    select, live = call(
        prepare_kernel,
        "prepare",
        (shape((rows, snap_count), bf16), shape((SLOTS, LANES), f32)),
        [SMEM, VMEM, VMEM],
        4 * rows * snap_count,
        2 * rows * snap_count,
    )(own.reshape(1), lengths, owners)
    partial, sent = project(snapshots, gathered, 2)
    swap = [(i, i ^ 1) for i in range(devices)]
    other = lax.ppermute(sent, "space", swap)
    kept_rows = rows // 2
    flops = rows * snap_count * modes
    given = call(
        give_kernel, "give", shape((kept_rows, modes), bf16), [VMEM] * 3, flops, 4 * rows * modes
    )(select, partial, other)
    near = [(2 * z + 1, 2 * (z ^ 1) + 1) for z in range(chips)]
    near += [(2 * z, 2 * ((((z + 1) ^ 1) - 1) % chips)) for z in range(chips)]
    given = lax.ppermute(given, "space", near)
    kept = call(
        keep_kernel, "keep", shape((kept_rows, modes), f32), [VMEM] * 3, 2 * flops, 4 * rows * modes
    )(select, partial, other)
    merged, mine = call(
        merge_kernel,
        "merge",
        (shape((kept_rows, modes), bf16), shape((SLOTS, modes), f32)),
        [SMEM, VMEM, VMEM],
        rows * modes,
        4 * rows * modes,
    )(own.reshape(1), kept, given)
    pairs = chips // 2
    order = [(i + FIRST_PAIR) % pairs for i in range(pairs)]
    along_z = [[2 * (2 * pair + p) + c for pair in order] for p in range(2) for c in range(2)]
    parts = lax.all_to_all(
        merged.reshape(pairs, SLOTS, -1), "space", 0, 0, axis_index_groups=along_z, tiled=True
    )
    term_count, table = picks()
    terms = modes + term_count
    gram, target = call(
        lambda *refs: library_kernel(devices / snap_count, *refs),
        "library",
        (shape((terms, terms), bf16), shape((terms, modes), bf16)),
        [SMEM] + [VMEM] * 4,
        2 * SLOTS * terms * (terms + modes),
        2 * terms * (terms + modes),
    )(own.reshape(1), parts, mine, live, jnp.asarray(table))
    return gram[None, None], target[None, None]


def solution(mesh):
    placed = (P("space", "tm"), P(("space", "tm"), None), P("tm", None), P("tm", None))
    return jax.shard_map(
        on_device,
        mesh=mesh,
        in_specs=placed,
        out_specs=(P("tm", "space", None, None), P("tm", "space", None, None)),
        check_vma=False,
    )
```

```python
import jax
import jax.numpy as jnp
import numpy as np
from jax import lax
from jax.experimental import pallas as pl
from jax.experimental.pallas import tpu as pltpu
from jax.sharding import PartitionSpec as P

QM = 16
SLOTS = 64
LANES = 128
FIRST_PAIR = (6, 5)
FIRST_TM = 10
f32 = jnp.float32
bf16 = jnp.bfloat16
i32 = jnp.int32
VMEM = pl.BlockSpec(memory_space=pltpu.VMEM)
SMEM = pl.BlockSpec(memory_space=pltpu.SMEM)


def rotated(chip, count):
    first = jnp.where(jnp.bitwise_and(chip, 1) == 0, FIRST_PAIR[0], FIRST_PAIR[1])
    return jnp.bitwise_and(jnp.right_shift(chip, 1) - first, count - 1)


def iota(shape, axis):
    return lax.broadcasted_iota(i32, shape, axis)


def prepare_kernel(own_ref, length_ref, owner_ref, select_ref, live_ref):
    own = own_ref[0]
    t = length_ref.shape[1]
    snap_count = select_ref.shape[1]
    ti, tj = iota((t, t), 0), iota((t, t), 1)
    length_row = jnp.broadcast_to(length_ref[...], (t, t))
    owner_row = jnp.broadcast_to(owner_ref[...], (t, t))
    length_col = jnp.sum(jnp.where(ti == tj, length_row, 0), axis=1, keepdims=True)
    owner_col = jnp.sum(jnp.where(ti == tj, owner_row, 0), axis=1, keepdims=True)
    same = owner_row == owner_col
    starts = jnp.sum(jnp.where(tj < ti, length_row, 0), axis=1, keepdims=True)
    offset = jnp.sum(jnp.where((tj < ti) & same, length_row, 0), axis=1, keepdims=True)
    chip = jnp.right_shift(owner_col, 1)
    across = jnp.bitwise_and(chip + jnp.right_shift(own, 1), 1)
    half = select_ref.shape[0] // (2 * SLOTS)
    place = across * half + rotated(chip, half)
    base = jnp.where(
        jnp.bitwise_and(owner_col, 1) == jnp.bitwise_and(own, 1),
        place * SLOTS + offset - starts,
        -2 * snap_count,
    )
    snap = iota((t, snap_count), 1)
    member = (snap >= starts) & (snap < starts + length_col)
    target = jnp.sum(jnp.where(member, base, 0), axis=0, keepdims=True) + iota((1, snap_count), 1)
    for at in range(0, select_ref.shape[0], SLOTS):
        slot = iota((SLOTS, snap_count), 0) + at
        select_ref[pl.ds(at, SLOTS), :] = jnp.where(slot == target, 1.0, 0.0).astype(bf16)
    row = slice(0, 1)
    offset_row = jnp.sum(jnp.where((ti < tj) & same, length_col, 0), axis=0, keepdims=True)
    mine = owner_row[row] == own
    total = jnp.sum(jnp.where(mine, length_row[row], 0), axis=1, keepdims=True)
    here = iota((SLOTS, t), 0)
    ends = mine & (here == offset_row + length_row[row] - 1)
    last = jnp.sum(jnp.where(ends, 1, 0), axis=1, keepdims=True)
    live = (iota((SLOTS, 1), 0) < total) & (last == 0)
    live_ref[...] = jnp.broadcast_to(jnp.where(live, 1.0, 0.0), (SLOTS, LANES))


def project_kernel(snapshots_ref, basis_ref, partial_ref, sent_ref):
    step = pl.program_id(0)
    blocks, width, modes = basis_ref.shape
    count = snapshots_ref.shape[0] // width
    turn = [jnp.bitwise_and(step * count + i - FIRST_TM, blocks - 1) for i in range(count)]
    basis = jnp.concatenate([basis_ref[i] for i in turn], axis=0)
    piece = lax.dot_general(
        basis, snapshots_ref[...], (((0,), (0,)), ((), ())), preferred_element_type=f32
    )

    @pl.when(step == 0)
    def _():
        partial_ref[...] = piece

    @pl.when(step > 0)
    def _():
        total = partial_ref[...] + piece
        partial_ref[...] = total
        high = total.astype(bf16)
        sent_ref[: total.shape[0], :] = high
        sent_ref[total.shape[0] :, :] = (total[:QM] - high[:QM].astype(f32)).astype(bf16)


def project(snapshots, basis, steps):
    cells, snap_count = snapshots.shape
    modes = basis.shape[2]
    heights = (modes, modes + QM)
    return pl.pallas_call(
        project_kernel,
        grid=(steps,),
        out_shape=tuple(jax.ShapeDtypeStruct((h, snap_count), kind) for h, kind in zip(heights, (f32, bf16))),
        in_specs=[
            pl.BlockSpec((cells // steps, snap_count), lambda i: (i, 0)),
            VMEM,
        ],
        out_specs=tuple(pl.BlockSpec((h, snap_count), lambda i: (0, 0)) for h in heights),
        compiler_params=pltpu.CompilerParams(vmem_limit_bytes=50 << 20),
        cost_estimate=pl.CostEstimate(
            flops=2 * cells * snap_count * modes, bytes_accessed=2 * cells * snap_count, transcendentals=0
        ),
        name="project",
    )(snapshots, basis)


NT = (((1,), (1,)), ((), ()))


def chip_sum(partial_ref, other_ref):
    modes = partial_ref.shape[0]
    total = partial_ref[...] + other_ref[:modes].astype(f32)
    lead = total[:QM] + other_ref[modes:].astype(f32)
    total = jnp.concatenate([lead, total[QM:]], axis=0)
    high = total.astype(bf16)
    return high, (total - high.astype(f32)).astype(bf16)


def give_kernel(select_ref, partial_ref, other_ref, given_ref):
    high, _ = chip_sum(partial_ref, other_ref)
    count = given_ref.shape[0]
    given_ref[...] = lax.dot_general(
        select_ref[count:, :], high, NT, preferred_element_type=f32
    ).astype(bf16)


def keep_kernel(select_ref, partial_ref, other_ref, kept_ref):
    high, low = chip_sum(partial_ref, other_ref)
    select = select_ref[: kept_ref.shape[0], :]
    kept_ref[...] = lax.dot_general(select, high, NT, preferred_element_type=f32) + lax.dot_general(
        select, low, NT, preferred_element_type=f32
    )


def merge_kernel(own_ref, kept_ref, given_ref, merged_ref, mine_ref):
    merged_ref[...] = (kept_ref[...] + given_ref[...].astype(f32)).astype(bf16)
    me = rotated(jnp.right_shift(own_ref[0], 1), kept_ref.shape[0] // SLOTS)
    at = pl.ds(pl.multiple_of(me * SLOTS, SLOTS), SLOTS)
    mine_ref[...] = kept_ref[at, :] + given_ref[at, :].astype(f32)


def library_kernel(weight_scale, own_ref, parts_ref, mine_ref, live_ref, pick_ref, gram_ref, target_ref):
    me = rotated(jnp.right_shift(own_ref[0], 1), parts_ref.shape[0])
    coords = mine_ref[...]
    for i in range(parts_ref.shape[0]):
        coords = coords + jnp.where(i == me, 0.0, parts_ref[i].astype(f32))
    modes = coords.shape[1]
    terms = pick_ref.shape[1] // 2
    both = jnp.dot(
        coords[:, :LANES], pick_ref[...], precision=lax.Precision.HIGHEST, preferred_element_type=f32
    )
    products = both[:, :terms] * both[:, terms:]
    theta = jnp.concatenate([coords, products], axis=1).astype(bf16)[:, : gram_ref.shape[0]]
    live = live_ref[:, :1].astype(bf16)
    weighted = theta * live
    row = iota((SLOTS, modes), 0)
    successor = jnp.where(row < SLOTS - 1, pltpu.roll(coords, SLOTS - 1, 0), 0.0).astype(bf16)
    dims = (((0,), (0,)), ((), ()))
    gram = lax.dot_general(weighted, theta, dims, preferred_element_type=f32) * weight_scale
    gram_ref[...] = gram.astype(bf16)
    target = lax.dot_general(weighted, successor, dims, preferred_element_type=f32) * weight_scale
    target_ref[...] = target.astype(bf16)


def call(kernel, name, outs, specs, flops, nbytes, mib=24, **more):
    return pl.pallas_call(
        kernel,
        out_shape=outs,
        in_specs=specs,
        out_specs=jax.tree.map(lambda _: VMEM, outs),
        compiler_params=pltpu.CompilerParams(vmem_limit_bytes=mib << 20),
        cost_estimate=pl.CostEstimate(flops=flops, bytes_accessed=nbytes, transcendentals=0),
        name=name,
        **more,
    )


def picks():
    first_mode, second_mode = np.triu_indices(QM)
    table = np.zeros((LANES, 4 * LANES), np.float32)
    for term, (a, b) in enumerate(zip(first_mode, second_mode)):
        table[a, term] = 1.0
        table[b, 2 * LANES + term] = 1.0
    return len(first_mode), table


def on_device(snapshots, basis, lengths, owners):
    cells, snap_count = snapshots.shape
    modes = basis.shape[1]
    devices = lax.axis_size("space")
    chips = devices // 2
    groups_tm = lax.axis_size("tm")
    own = lax.axis_index("space")
    rows = chips * SLOTS
    shape = jax.ShapeDtypeStruct

    copies = jnp.broadcast_to(basis[None], (groups_tm,) + basis.shape)
    order = [(i + FIRST_TM) % groups_tm for i in range(groups_tm)]
    gathered = lax.all_to_all(copies, "tm", 0, 0, axis_index_groups=[order], tiled=True)
    select, live = call(
        prepare_kernel,
        "prepare",
        (shape((rows, snap_count), bf16), shape((SLOTS, LANES), f32)),
        [SMEM, VMEM, VMEM],
        4 * rows * snap_count,
        2 * rows * snap_count,
    )(own.reshape(1), lengths, owners)
    partial, sent = project(snapshots, gathered, 2)
    swap = [(i, i ^ 1) for i in range(devices)]
    other = lax.ppermute(sent, "space", swap)
    kept_rows = rows // 2
    flops = rows * snap_count * modes
    given = call(
        give_kernel, "give", shape((kept_rows, modes), bf16), [VMEM] * 3, flops, 4 * rows * modes
    )(select, partial, other)
    near = [(2 * z + 1, 2 * (z ^ 1) + 1) for z in range(chips)]
    near += [(2 * z, 2 * ((((z + 1) ^ 1) - 1) % chips)) for z in range(chips)]
    given = lax.ppermute(given, "space", near)
    kept = call(
        keep_kernel, "keep", shape((kept_rows, modes), f32), [VMEM] * 3, 2 * flops, 4 * rows * modes
    )(select, partial, other)
    merged, mine = call(
        merge_kernel,
        "merge",
        (shape((kept_rows, modes), bf16), shape((SLOTS, modes), f32)),
        [SMEM, VMEM, VMEM],
        rows * modes,
        4 * rows * modes,
    )(own.reshape(1), kept, given)
    pairs = chips // 2
    order = [[(i + first) % pairs for i in range(pairs)] for first in FIRST_PAIR]
    along_z = [[2 * (2 * pair + p) + c for pair in order[p]] for p in range(2) for c in range(2)]
    parts = lax.all_to_all(
        merged.reshape(pairs, SLOTS, -1), "space", 0, 0, axis_index_groups=along_z, tiled=True
    )
    term_count, table = picks()
    terms = modes + term_count
    gram, target = call(
        lambda *refs: library_kernel(devices / snap_count, *refs),
        "library",
        (shape((terms, terms), bf16), shape((terms, modes), bf16)),
        [SMEM] + [VMEM] * 4,
        2 * SLOTS * terms * (terms + modes),
        2 * terms * (terms + modes),
    )(own.reshape(1), parts, mine, live, jnp.asarray(table))
    return gram[None, None], target[None, None]


def solution(mesh):
    placed = (P("space", "tm"), P(("space", "tm"), None), P("tm", None), P("tm", None))
    return jax.shard_map(
        on_device,
        mesh=mesh,
        in_specs=placed,
        out_specs=(P("tm", "space", None, None), P("tm", "space", None, None)),
        check_vma=False,
    )
```
